32 devices in a mesh: groups: 2 (over y), chan: 4 (over z), tm: 2 (over x), src: 2 (over core).
Axes of the slice: x: 2, y: 2, z: 4, core: 2. Of those that a mesh axis runs over, the one named last changes fastest.
Arguments:
- record: float32 [8192, 512], P(('groups', 'chan', 'src'), 'tm'), parts along dimension 0, may hold values from -6 to 6
- fir_taps: float32 [4, 128], replicated, may hold values from -0.5 to 0.5
- chan_table: int32 [4096], P(('chan', 'src')), may hold values from 0 to 3
- steering: bfloat16 [32, 256, 128], P(('chan', 'src')), may hold values from -0.375 to 0.375
- pair_block: int32 [64], P(('chan', 'src')), may hold values from 0 to 3
- pair_owner: int32 [64, 1], P(('chan', 'src')), may hold values from 0 to 7; in each aligned block of 8 rows (0 to 7, 8 to 15, ...) at most 2 rows name the same one
- pair_sub: int32 [64], P(('chan', 'src')), may hold values from 0 to 3
- pair_delay: int32 [64], P(('chan', 'src')), may hold values from 1 to 254
- pair_frac: int32 [64], P(('chan', 'src')), may hold values from 0 to 15
Outputs:
- beam: float32 [16384, 512], P(('groups', 'chan', 'src'), 'tm'), parts along dimension 0
The draws below stay inside these ranges and needn't reach their ends.
There are 2 independent parts, one for each index of `groups`. The reference program is written for one: setup_inputs(seed, part) draws one part's arguments, and reference() takes and returns one part's arrays. A program takes and returns all parts, laid end to end along the dimension named above; an argument that names none is the same for every part. Nothing has to cross between parts.
Inputs may be any that keep to these rules, and one draw needn't show every extreme that they name: `pair_owner`: in the rows of one device (aligned blocks of 8 rows) no owner is named more than 2 times, and in every draw some owner is named exactly 2 times in some such block; every owner is named somewhere.
All inputs are finite; a program needn't handle non-finite values.
Results may differ from the reference program's by a relative error of at most 0.0029.
Values may be sent and summed in bfloat16 or wider, within the bound.
A program may use at most 128 MiB of HBM per device.

```python
import math
import jax
import jax.numpy as jnp
import numpy as np
from jax import lax

CHANNEL_PER_BLK = 128
POINTS_PER_BLOCK = 256
TAPS = 128
WINDOW_SAMPLES = 512
NTAB = 4
NFRAC = 16
CB_DEV = 4
SOURCE_BLK_OWNED = 4
PAIR_LIMIT = 2
SEGMENT_SAMPLES = 256
PAIRS_DEV = 8
CHANNELS = 4096
SOURCE_BLOCKS = 32
PAIRS = 64
N_CHAN = 4
N_SRC = 2


def with_ends(entries, stream_key, low, high):
    dims = entries.shape
    spot = [jax.random.randint(jax.random.fold_in(stream_key, axis), (), 0, dims[axis]) for axis in range(len(dims))]
    entries = entries.at[tuple(spot)].set(low)
    longest = dims.index(max(dims))
    spot[longest] = (spot[longest] + 1) % dims[longest]
    return entries.at[tuple(spot)].set(high)


def block_scale(own_key, shape, shards, low, top_value):
    loudness, own = 1.0, jax.random.fold_in(own_key, 6)
    for dim, shards_of in shards:
        draws = jnp.exp(jax.random.uniform(jax.random.fold_in(own, dim), (shards_of,), jnp.float32, low / len(shards), top_value / len(shards)))
        loudness = loudness * jnp.repeat(draws, shape[dim] // shards_of).reshape([-1 if axis == dim else 1 for axis in range(len(shape))])
    return loudness


def assign_block(stream_key, own, number, rows, count, top, limit, skew):
    sequence = jax.random.permutation(stream_key, count)
    heavy_load, common = load_shares(count, rows * top, limit, skew, True), load_shares(count, rows * top, limit, skew, False)
    places = jnp.arange(count)

    def named(tallies, rotation):
        used = int((tallies > 0).sum())
        fixed = max(1, used // 4)
        moved = fixed + (places - fixed + rotation * (used - fixed)) % max(1, count - fixed)
        return jnp.zeros((count,), jnp.int32).at[sequence[jnp.where(places < fixed, places, moved)]].set(jnp.asarray(tallies, jnp.int32))

    tallies = jnp.where(number % 4 == 0, named(heavy_load, number // 4), named(common, number - number // 4 - 1))
    mixed = jax.random.permutation(jax.random.fold_in(own, 3), count)
    giver, taker = mixed[0:count // 2 * 2:2], mixed[1:count // 2 * 2:2]
    margin = jnp.minimum(tallies[giver] - 1, limit - tallies[taker]) // 2
    margin = jnp.where((giver == sequence[0]) | (taker == sequence[0]) | (tallies[taker] == 0), 0, jnp.maximum(margin, 0))
    moved = jax.random.randint(jax.random.fold_in(own, 4), (count // 2,), 0, 1 << 20) % (margin + 1)
    tallies = tallies.at[giver].add(-moved).at[taker].add(moved)
    members = jnp.searchsorted(jnp.cumsum(tallies), jnp.arange(rows * top), side="right").astype(jnp.int32)
    grid = members.reshape(top, rows).T
    grid = grid[jax.random.permutation(jax.random.fold_in(own, 1), rows)]
    rotation = jax.random.randint(jax.random.fold_in(own, 2), (rows, 1), 0, top)
    return jnp.take_along_axis(grid, (jnp.arange(top)[None, :] + rotation) % top, axis=1)


def load_shares(count, total, most, lean, full):
    loads = [(1 << 20) // math.isqrt(standing ** lean) + 1 for standing in range(1, count + 1)]
    largest = most if full else min(most, max(-(-total // count), total * loads[0] // sum(loads)))
    least = 1 if total - largest >= count - 1 else 0
    holding, surplus = [largest] + [least] * (count - 1), total - largest - least * (count - 1)
    while surplus > 0:
        movable = [i for i in range(1, count) if holding[i] < largest] or [i for i in range(1, count) if holding[i] < most]
        mass, remaining = sum([loads[i] for i in movable]), surplus
        for i in movable:
            more = min(most - holding[i], max(1, remaining * loads[i] // mass), surplus)
            holding[i] = holding[i] + more
            surplus = surplus - more
    return np.array(holding)


def bell_draw(own_key, dims, scale, bound, pieces=(), kind=jnp.bfloat16):
    entries = scale * jax.random.normal(own_key, dims, jnp.float32)
    if pieces:
        entries = entries * block_scale(own_key, dims, pieces, -0.22, 0.18)
    return jnp.clip(entries, -bound, bound).astype(kind)


def setup_inputs(seed: int = 0, part: int = 0) -> dict:
    seeds = jax.random.split(jax.random.key(seed), 10)
    part_keys = jax.random.split(jax.random.fold_in(seeds[9], part), 10)
    record = bell_draw(part_keys[0], (CHANNELS, WINDOW_SAMPLES), 1.0, 6.0, ((0, 8), (1, 2)), jnp.float32)
    fir_taps = bell_draw(seeds[1], (NTAB, TAPS), TAPS ** -0.5, 0.5, (), jnp.float32)
    chan_table = with_ends(jax.random.randint(seeds[2], (CHANNELS,), 0, NTAB), jax.random.fold_in(seeds[2], 1), 0, NTAB - 1).astype(jnp.int32)
    steering = bell_draw(seeds[3], (SOURCE_BLOCKS, POINTS_PER_BLOCK, CHANNEL_PER_BLK), (CHANNEL_PER_BLK * PAIR_LIMIT * N_CHAN * N_SRC // (2 * SOURCE_BLK_OWNED)) ** -0.5, 0.375, ((0, 8),))
    pair_block = with_ends(jax.random.randint(seeds[4], (PAIRS,), 0, CB_DEV), jax.random.fold_in(seeds[4], 1), 0, CB_DEV - 1).astype(jnp.int32)
    pair_owner_keys = jax.random.split(jax.random.fold_in(seeds[5], 1), PAIRS // PAIRS_DEV)
    pair_owner_turns = jax.random.permutation(jax.random.fold_in(seeds[5], 3), PAIRS // PAIRS_DEV)
    pair_owner = jax.vmap(lambda own, number: assign_block(jax.random.fold_in(seeds[5], 2), own, number, PAIRS_DEV, N_CHAN * N_SRC, 1, PAIR_LIMIT, 2))(pair_owner_keys, pair_owner_turns).reshape((PAIRS, 1))
    pair_sub = with_ends(jax.random.randint(seeds[6], (PAIRS,), 0, SOURCE_BLK_OWNED), jax.random.fold_in(seeds[6], 1), 0, SOURCE_BLK_OWNED - 1).astype(jnp.int32)
    pair_delay = with_ends(jax.random.randint(seeds[7], (PAIRS,), 1, SEGMENT_SAMPLES - 1), jax.random.fold_in(seeds[7], 1), 1, (SEGMENT_SAMPLES - 1) - 1).astype(jnp.int32)
    pair_frac = with_ends(jax.random.randint(seeds[8], (PAIRS,), 0, NFRAC), jax.random.fold_in(seeds[8], 1), 0, NFRAC - 1).astype(jnp.int32)
    return {"record": record, "fir_taps": fir_taps, "chan_table": chan_table, "steering": steering, "pair_block": pair_block, "pair_owner": pair_owner, "pair_sub": pair_sub, "pair_delay": pair_delay, "pair_frac": pair_frac}


def lagrange(position):
    first = -position * (position - 1.0) * (position - 2.0) / 6.0
    second = (position + 1.0) * (position - 1.0) * (position - 2.0) / 2.0
    third = -(position + 1.0) * position * (position - 2.0) / 2.0
    fourth = (position + 1.0) * position * (position - 1.0) / 6.0
    return jnp.stack([first, second, third, fourth], axis=-1)


def reference(record, fir_taps, chan_table, steering, pair_block, pair_owner, pair_sub, pair_delay, pair_frac):
    channel_list = record.shape[0]
    select = (chan_table[:, None] == jnp.arange(NTAB, dtype=jnp.int32)[None, :]).astype(jnp.float32)
    chan_taps = jnp.dot(select, fir_taps, precision=lax.Precision.HIGHEST)
    padded = jnp.pad(record, ((0, 0), (TAPS - 1, 0)))

    def add_tap(step, total):
        column = lax.dynamic_slice_in_dim(chan_taps, step, 1, 1)
        window = lax.dynamic_slice_in_dim(padded, TAPS - 1 - step, WINDOW_SAMPLES, 1)
        return total + column * window

    filtered_trace = lax.fori_loop(0, TAPS, add_tap, jnp.zeros((channel_list, WINDOW_SAMPLES), jnp.float32))
    extended_trace = jnp.pad(filtered_trace, ((0, 0), (0, SEGMENT_SAMPLES))).reshape(channel_list // CHANNEL_PER_BLK, CHANNEL_PER_BLK, WINDOW_SAMPLES + SEGMENT_SAMPLES)
    weights = lagrange(pair_frac.astype(jnp.float32) / NFRAC)
    pair_count = pair_block.shape[0]
    lister = jnp.arange(pair_count, dtype=jnp.int32) // PAIRS_DEV
    chan_block = (lister * CB_DEV + pair_block).astype(jnp.int32)
    source_block = (pair_owner[:, 0] * SOURCE_BLK_OWNED + pair_sub).astype(jnp.int32)

    def accumulate_pair(stacked_sums, index):
        rows = extended_trace[chan_block[index]]
        window = lax.dynamic_slice_in_dim(rows, (pair_delay[index] - 1).astype(jnp.int32), WINDOW_SAMPLES + 3, 1)
        weight = weights[index]
        mixed = weight[0] * window[:, 0:WINDOW_SAMPLES] + weight[1] * window[:, 1:WINDOW_SAMPLES + 1]
        mixed = mixed + weight[2] * window[:, 2:WINDOW_SAMPLES + 2] + weight[3] * window[:, 3:WINDOW_SAMPLES + 3]
        rounded = lax.optimization_barrier(mixed.astype(jnp.bfloat16)).astype(jnp.float32)
        return stacked_sums.at[source_block[index]].add(rounded), None

    block_count = steering.shape[0]
    stacked_sums, unused_value = lax.scan(accumulate_pair, jnp.zeros((block_count, CHANNEL_PER_BLK, WINDOW_SAMPLES), jnp.float32), jnp.arange(pair_count, dtype=jnp.int32))
    beam = jnp.einsum("bxc,bct->bxt", steering.astype(jnp.float32), stacked_sums, precision=lax.Precision.HIGHEST)
    return beam.reshape(block_count * POINTS_PER_BLOCK, WINDOW_SAMPLES)
```

```python
import functools

import jax
import jax.numpy as jnp
from jax import lax
from jax.experimental import pallas as pl
from jax.experimental.pallas import tpu as pltpu
from jax.sharding import PartitionSpec as P

NFRAC = 16
GROUPS = 4
MESH = pl.DeviceIdType.MESH


def split(value):
    high = value.astype(jnp.bfloat16)
    return high, (value - high.astype(jnp.float32)).astype(jnp.bfloat16)


def mm(a, b):
    return jnp.dot(a, b, preferred_element_type=jnp.float32)


def kernel(
    dims,
    block_ref,
    owner_ref,
    sub_ref,
    delay_ref,
    frac_ref,
    record,
    taps_ref,
    table_ref,
    steer_ref,
    beam_ref,
    prev,
    after,
    band_hi,
    band_lo,
    tab,
    filt,
    shifted,
    out_slots,
    in_slots,
    out_label,
    in_label,
    sums,
    slot_pair,
    prev_send,
    prev_recv,
    after_send,
    after_recv,
    slot_send,
    slot_recv,
    label_send,
    label_recv,
):
    nchan, nsrc, ntm = dims
    owners = nchan * nsrc
    blocks, block_rows, seg = record.shape
    ntab, ntaps = taps_ref.shape
    pairs = block_ref.shape[0]
    cap = out_slots.shape[1]
    targets = steer_ref.shape[0]
    points = steer_ref.shape[1]
    step_rows = block_rows // GROUPS
    rows = blocks * step_rows
    me = lax.axis_index("chan") * nsrc + lax.axis_index("src")
    tm = lax.axis_index("tm")

    def place(owner):
        return {"chan": owner // nsrc, "src": owner % nsrc}

    barrier = pltpu.get_barrier_semaphore()

    @pl.when(tm > 0)
    def _():
        pl.semaphore_signal(barrier, inc=1, device_id={"tm": tm - 1}, device_id_type=MESH)

    @pl.when(tm < ntm - 1)
    def _():
        pl.semaphore_signal(barrier, inc=1, device_id={"tm": tm + 1}, device_id_type=MESH)

    def greet(i, carry):
        pl.semaphore_signal(
            barrier, inc=1, device_id=place((me + i) % owners), device_id_type=MESH
        )
        return carry

    lax.fori_loop(1, owners, greet, 0)

    for m in range(ntab):
        row = jnp.concatenate([taps_ref[m : m + 1, :], jnp.zeros((1, ntaps), jnp.float32)], axis=1)
        full = jnp.broadcast_to(row, (2 * ntaps, 2 * ntaps))
        rolled = pltpu.roll(full, ntaps, 1, stride=1, stride_axis=0)[:, :ntaps]
        high, low = split(rolled)
        band_hi[:, m * ntaps : (m + 1) * ntaps] = high
        band_lo[:, m * ntaps : (m + 1) * ntaps] = low

    @pl.when(tm == 0)
    def _():
        prev[...] = jnp.zeros_like(prev)

    @pl.when(tm == ntm - 1)
    def _():
        after[...] = jnp.zeros_like(after)

    pl.semaphore_wait(
        barrier,
        owners - 1 + jnp.where(tm > 0, 1, 0) + jnp.where(tm < ntm - 1, 1, 0),
    )

    def part(r):
        return pl.ds(pl.multiple_of(r * step_rows, step_rows), step_rows)

    def to_prev(r):
        return pltpu.make_async_remote_copy(
            src_ref=record.at[:, part(r), pl.ds(seg - ntaps, ntaps)],
            dst_ref=prev.at[:, part(r), :],
            send_sem=prev_send.at[r],
            recv_sem=prev_recv.at[r],
            device_id={"tm": tm + 1},
            device_id_type=MESH,
        )

    def to_after(r):
        return pltpu.make_async_remote_copy(
            src_ref=record.at[:, part(r), :],
            dst_ref=after.at[:, part(r), :],
            send_sem=after_send.at[r],
            recv_sem=after_recv.at[r],
            device_id={"tm": tm - 1},
            device_id_type=MESH,
        )

    def slots_to(r, other, landing):
        return pltpu.make_async_remote_copy(
            src_ref=out_slots.at[other, :, part(r), :],
            dst_ref=in_slots.at[landing, :, part(r), :],
            send_sem=slot_send.at[r, other],
            recv_sem=slot_recv.at[r, landing],
            device_id=place(other),
            device_id_type=MESH,
        )

    def label_to(other, landing):
        return pltpu.make_async_remote_copy(
            src_ref=out_label.at[other],
            dst_ref=in_label.at[landing],
            send_sem=label_send.at[other],
            recv_sem=label_recv.at[landing],
            device_id=place(other),
            device_id_type=MESH,
        )

    for r in range(GROUPS):

        @pl.when(tm > 0)
        def _():
            to_after(r).start()

        @pl.when(tm < ntm - 1)
        def _():
            to_prev(r).start()

    for g in range(blocks):
        tab[g] = jnp.broadcast_to(table_ref[g : g + 1, :], (block_rows, block_rows)).T

    def slots_of(owner, carry):
        def look(p, found):
            hit = owner_ref[p] == owner
            count = found[0]
            named = [
                jnp.where(jnp.logical_and(hit, count == k), p, found[1 + k]) for k in range(cap)
            ]
            return (count + jnp.where(hit, 1, 0), *named)

        found = lax.fori_loop(0, pairs, look, (0,) + (-1,) * cap, unroll=min(pairs, 8))
        line = lax.broadcasted_iota(jnp.int32, out_label.shape[1:], 0)
        labels = jnp.full(out_label.shape[1:], -1.0, jnp.float32)
        for k in range(cap):
            pair = jnp.maximum(found[1 + k], 0)
            slot_pair[owner * cap + k] = pair
            name = jnp.where(found[1 + k] >= 0, sub_ref[pair], -1).astype(jnp.float32)
            labels = jnp.where(line == k, name, labels)
        out_label[owner] = labels
        return carry

    lax.fori_loop(0, owners, slots_of, 0)

    def send_label(i, carry):
        label_to((me + i) % owners, me).start()
        return carry

    lax.fori_loop(1, owners, send_label, 0)

    def produce(r, carry):
        @pl.when(tm > 0)
        def _():
            to_prev(r).wait_recv()

        @pl.when(tm < ntm - 1)
        def _():
            to_after(r).wait_recv()

        window = jnp.concatenate(
            [
                prev[:, part(r), :].reshape(rows, ntaps),
                record[:, part(r), :].reshape(rows, seg),
                after[:, part(r), :].reshape(rows, seg),
            ],
            axis=1,
        )
        high, low = split(window)
        steps = 2 * seg // ntaps
        lhs_hi = jnp.concatenate([high[:, j * ntaps : (j + 2) * ntaps] for j in range(steps)], axis=0)
        lhs_lo = jnp.concatenate([low[:, j * ntaps : (j + 2) * ntaps] for j in range(steps)], axis=0)
        every = mm(lhs_lo, band_hi[...]) + mm(lhs_hi, band_lo[...]) + mm(lhs_hi, band_hi[...])
        which = tab[:, part(r), :].reshape(rows, block_rows)
        inside = jnp.where(tm < ntm - 1, 1.0, 0.0)
        for j in range(steps):
            own = every[j * rows : (j + 1) * rows]
            value = own[:, :ntaps]
            for m in range(1, ntab):
                value = jnp.where(which == m, own[:, m * ntaps : (m + 1) * ntaps], value)
            if j >= seg // ntaps:
                value = value * inside
            filt[:, :, j * ntaps : (j + 1) * ntaps] = value.reshape(blocks, step_rows, ntaps)

        def one_pair(p, c):
            mu = jnp.full((1, seg), frac_ref[p].astype(jnp.float32)) / NFRAC
            first = -mu * (mu - 1.0) * (mu - 2.0) / 6.0
            second = (mu + 1.0) * (mu - 1.0) * (mu - 2.0) / 2.0
            third = -(mu + 1.0) * mu * (mu - 2.0) / 2.0
            fourth = (mu + 1.0) * mu * (mu - 1.0) / 6.0
            source = filt[block_ref[p]]
            base = pltpu.roll(source, 2 * seg - (delay_ref[p] - 1), 1)
            mixed = first * base[:, :seg]
            mixed = mixed + second * pltpu.roll(base, 2 * seg - 1, 1)[:, :seg]
            mixed = mixed + third * pltpu.roll(base, 2 * seg - 2, 1)[:, :seg]
            mixed = mixed + fourth * pltpu.roll(base, 2 * seg - 3, 1)[:, :seg]
            shifted[p] = mixed.astype(jnp.bfloat16)
            return c

        lax.fori_loop(0, pairs, one_pair, 0, unroll=min(pairs, 4))

        def ship(i, c):
            other = (me + owners // 2 + i) % owners
            for k in range(cap):
                out_slots[other, k, part(r), :] = shifted[slot_pair[other * cap + k]]

            @pl.when(other != me)
            def _():
                slots_to(r, other, me).start()

            return c

        lax.fori_loop(0, owners, ship, 0)
        return carry

    lax.fori_loop(0, GROUPS, produce, 0)

    def wait_label(i, carry):
        source = (me + i) % owners
        label_to(source, source).wait_recv()
        return carry

    lax.fori_loop(1, owners, wait_label, 0)

    def add(total, values, labels):
        for k in range(cap):
            name = jnp.concatenate([labels[k : k + 1, :]] * (seg // labels.shape[1]), axis=1)
            value = values[k].astype(jnp.float32)
            total = [
                total[b] + value * jnp.where(name == float(b), 1.0, 0.0) for b in range(targets)
            ]
        return total

    def gather(r, carry):
        total = [jnp.zeros((step_rows, seg), jnp.float32)] * targets
        total = add(total, out_slots[me, :, part(r), :], out_label[me])

        def one_source(i, running):
            source = (me + i) % owners
            slots_to(r, source, source).wait_recv()
            return tuple(add(list(running), in_slots[source, :, part(r), :], in_label[source]))

        total = lax.fori_loop(1, owners, one_source, tuple(total))
        for b in range(targets):
            sums[b, part(r), :] = total[b]
        return carry

    lax.fori_loop(0, GROUPS, gather, 0)

    for b in range(targets):
        high, low = split(sums[b])
        beam_ref[b * points : (b + 1) * points, :] = mm(steer_ref[b], high) + mm(steer_ref[b], low)

    def finish(i, carry):
        other = (me + i) % owners
        label_to(other, me).wait_send()
        for r in range(GROUPS):
            slots_to(r, other, me).wait_send()
        return carry

    lax.fori_loop(1, owners, finish, 0)
    for r in range(GROUPS):

        @pl.when(tm > 0)
        def _():
            to_after(r).wait_send()

        @pl.when(tm < ntm - 1)
        def _():
            to_prev(r).wait_send()


def solution(mesh):
    nchan, nsrc, ntm = mesh.shape["chan"], mesh.shape["src"], mesh.shape["tm"]
    owners = nchan * nsrc

    def local(
        record, fir_taps, chan_table, steering, pair_block, pair_owner, pair_sub, pair_delay, pair_frac
    ):
        channels, seg = record.shape
        ntab, ntaps = fir_taps.shape
        targets, points, block_rows = steering.shape
        blocks = channels // block_rows
        pairs = pair_block.shape[0]
        cap = 2 * pairs // owners
        step_rows = block_rows // GROUPS
        smem = pl.BlockSpec(memory_space=pltpu.SMEM)
        vmem = pl.BlockSpec(memory_space=pltpu.VMEM)
        dma = pltpu.SemaphoreType.DMA
        return pl.pallas_call(
            functools.partial(kernel, (nchan, nsrc, ntm)),
            out_shape=jax.ShapeDtypeStruct((targets * points, seg), jnp.float32),
            in_specs=[smem] * 5 + [vmem] * 4,
            out_specs=vmem,
            scratch_shapes=[
                pltpu.VMEM((blocks, block_rows, ntaps), jnp.float32),
                pltpu.VMEM((blocks, block_rows, seg), jnp.float32),
                pltpu.VMEM((2 * ntaps, ntab * ntaps), jnp.bfloat16),
                pltpu.VMEM((2 * ntaps, ntab * ntaps), jnp.bfloat16),
                pltpu.VMEM((blocks, block_rows, block_rows), jnp.int32),
                pltpu.VMEM((blocks, step_rows, 2 * seg), jnp.float32),
                pltpu.VMEM((pairs, step_rows, seg), jnp.bfloat16),
                pltpu.VMEM((owners, cap, block_rows, seg), jnp.bfloat16),
                pltpu.VMEM((owners, cap, block_rows, seg), jnp.bfloat16),
                pltpu.VMEM((owners, 8, 128), jnp.float32),
                pltpu.VMEM((owners, 8, 128), jnp.float32),
                pltpu.VMEM((targets, block_rows, seg), jnp.float32),
                pltpu.SMEM((owners * cap,), jnp.int32),
                dma((GROUPS,)),
                dma((GROUPS,)),
                dma((GROUPS,)),
                dma((GROUPS,)),
                dma((GROUPS, owners)),
                dma((GROUPS, owners)),
                dma((owners,)),
                dma((owners,)),
            ],
            compiler_params=pltpu.CompilerParams(collective_id=0, has_side_effects=True),
        )(
            pair_block,
            pair_owner.reshape(pairs),
            pair_sub,
            pair_delay,
            pair_frac,
            record.reshape(blocks, block_rows, seg),
            fir_taps,
            chan_table.reshape(blocks, block_rows),
            steering,
        )

    in_specs = (
        P(("groups", "chan", "src"), "tm"),
        P(),
        P(("chan", "src")),
        P(("chan", "src"), None, None),
        P(("chan", "src")),
        P(("chan", "src"), None),
        P(("chan", "src")),
        P(("chan", "src")),
        P(("chan", "src")),
    )
    out_specs = P(("groups", "chan", "src"), "tm")
    return jax.shard_map(local, mesh=mesh, in_specs=in_specs, out_specs=out_specs, check_vma=False)
```

```python
import functools

import jax
import jax.numpy as jnp
from jax import lax
from jax.experimental import pallas as pl
from jax.experimental.pallas import tpu as pltpu
from jax.sharding import PartitionSpec as P

NFRAC = 16
GROUPS = 4
PARTS = 8
LAG = 2
MORE = 1
MESH = pl.DeviceIdType.MESH


def split(value):
    high = value.astype(jnp.bfloat16)
    return high, (value - high.astype(jnp.float32)).astype(jnp.bfloat16)


def mm(a, b):
    return jnp.dot(a, b, preferred_element_type=jnp.float32)


def kernel(
    dims,
    block_ref,
    owner_ref,
    sub_ref,
    delay_ref,
    frac_ref,
    record,
    taps_ref,
    table_ref,
    steer_ref,
    beam_ref,
    prev,
    after,
    band_hi,
    band_lo,
    tab,
    filt,
    shifted,
    out_slots,
    in_slots,
    out_label,
    in_label,
    sums,
    slot_pair,
    prev_send,
    prev_recv,
    after_send,
    after_recv,
    slot_send,
    slot_recv,
    label_send,
    label_recv,
):
    nchan, nsrc, ntm = dims
    owners = nchan * nsrc
    blocks, block_rows, seg = record.shape
    ntab, ntaps = taps_ref.shape
    pairs = block_ref.shape[0]
    cap = out_slots.shape[1]
    targets = steer_ref.shape[0]
    points = steer_ref.shape[1]
    step_rows = block_rows // GROUPS
    rows = blocks * step_rows
    me = lax.axis_index("chan") * nsrc + lax.axis_index("src")
    tm = lax.axis_index("tm")

    def place(owner):
        return {"chan": owner // nsrc, "src": owner % nsrc}

    barrier = pltpu.get_barrier_semaphore()

    @pl.when(tm > 0)
    def _():
        pl.semaphore_signal(barrier, inc=1, device_id={"tm": tm - 1}, device_id_type=MESH)

    @pl.when(tm < ntm - 1)
    def _():
        pl.semaphore_signal(barrier, inc=1, device_id={"tm": tm + 1}, device_id_type=MESH)

    def greet(i, carry):
        pl.semaphore_signal(
            barrier, inc=1, device_id=place((me + i) % owners), device_id_type=MESH
        )
        return carry

    lax.fori_loop(1, owners, greet, 0)

    build_band(taps_ref, band_hi, band_lo)

    @pl.when(tm == 0)
    def _():
        prev[...] = jnp.zeros_like(prev)

    @pl.when(tm == ntm - 1)
    def _():
        after[...] = jnp.zeros_like(after)

    pl.semaphore_wait(
        barrier,
        owners - 1 + jnp.where(tm > 0, 1, 0) + jnp.where(tm < ntm - 1, 1, 0),
    )

    def part(r):
        return pl.ds(pl.multiple_of(r * step_rows, step_rows), step_rows)

    def to_prev(r):
        return pltpu.make_async_remote_copy(
            src_ref=record.at[:, part(r), pl.ds(seg - ntaps, ntaps)],
            dst_ref=prev.at[:, part(r), :],
            send_sem=prev_send.at[r],
            recv_sem=prev_recv.at[r],
            device_id={"tm": tm + 1},
            device_id_type=MESH,
        )

    def to_after(r):
        return pltpu.make_async_remote_copy(
            src_ref=record.at[:, part(r), :],
            dst_ref=after.at[:, part(r), :],
            send_sem=after_send.at[r],
            recv_sem=after_recv.at[r],
            device_id={"tm": tm - 1},
            device_id_type=MESH,
        )

    def slots_to(r, other, landing):
        return pltpu.make_async_remote_copy(
            src_ref=out_slots.at[other, :, part(r), :],
            dst_ref=in_slots.at[landing, :, part(r), :],
            send_sem=slot_send.at[r, other],
            recv_sem=slot_recv.at[r, landing],
            device_id=place(other),
            device_id_type=MESH,
        )

    def label_to(other, landing):
        return pltpu.make_async_remote_copy(
            src_ref=out_label.at[other],
            dst_ref=in_label.at[landing],
            send_sem=label_send.at[other],
            recv_sem=label_recv.at[landing],
            device_id=place(other),
            device_id_type=MESH,
        )

    for r in range(GROUPS):

        @pl.when(tm > 0)
        def _():
            to_after(r).start()

        @pl.when(tm < ntm - 1)
        def _():
            to_prev(r).start()

    for g in range(blocks):
        tab[g] = jnp.broadcast_to(table_ref[g : g + 1, :], (block_rows, block_rows)).T

    def slots_of(owner, carry):
        def look(p, found):
            hit = owner_ref[p] == owner
            count = found[0]
            named = [
                jnp.where(jnp.logical_and(hit, count == k), p, found[1 + k]) for k in range(cap)
            ]
            return (count + jnp.where(hit, 1, 0), *named)

        found = lax.fori_loop(0, pairs, look, (0,) + (-1,) * cap, unroll=min(pairs, 8))
        line = lax.broadcasted_iota(jnp.int32, out_label.shape[1:], 0)
        labels = jnp.full(out_label.shape[1:], -1.0, jnp.float32)
        for k in range(cap):
            pair = jnp.maximum(found[1 + k], 0)
            slot_pair[owner * cap + k] = pair
            name = jnp.where(found[1 + k] >= 0, sub_ref[pair], -1).astype(jnp.float32)
            labels = jnp.where(line == k, name, labels)
        out_label[owner] = labels
        return carry

    lax.fori_loop(0, owners, slots_of, 0)

    def send_label(i, carry):
        label_to((me + i) % owners, me).start()
        return carry

    lax.fori_loop(1, owners, send_label, 0)

    def produce(r, carry):
        @pl.when(tm > 0)
        def _():
            to_prev(r).wait_recv()

        @pl.when(tm < ntm - 1)
        def _():
            to_after(r).wait_recv()

        window = jnp.concatenate(
            [
                prev[:, part(r), :].reshape(rows, ntaps),
                record[:, part(r), :].reshape(rows, seg),
                after[:, part(r), :].reshape(rows, seg),
            ],
            axis=1,
        )
        inside = jnp.where(tm < ntm - 1, 1.0, 0.0)
        which = tab[:, part(r), :].reshape(rows, block_rows)
        band_filter(window, band_hi, band_lo, which, inside, seg, ntab, filt)

        def one_pair(p, c):
            shifted[p] = shift_pair(filt[block_ref[p]], delay_ref[p], frac_ref[p], seg)
            return c

        lax.fori_loop(0, pairs, one_pair, 0, unroll=min(pairs, 4))

        def ship(i, c):
            other = (me + owners // 2 + i) % owners
            for k in range(cap):
                out_slots[other, k, part(r), :] = shifted[slot_pair[other * cap + k]]

            @pl.when(other != me)
            def _():
                slots_to(r, other, me).start()

            return c

        lax.fori_loop(0, owners, ship, 0)
        return carry

    lax.fori_loop(0, GROUPS, produce, 0)

    def wait_label(i, carry):
        source = (me + i) % owners
        label_to(source, source).wait_recv()
        return carry

    lax.fori_loop(1, owners, wait_label, 0)

    def add(total, values, labels):
        for k in range(cap):
            name = jnp.concatenate([labels[k : k + 1, :]] * (seg // labels.shape[1]), axis=1)
            value = values[k].astype(jnp.float32)
            total = [
                total[b] + value * jnp.where(name == float(b), 1.0, 0.0) for b in range(targets)
            ]
        return total

    def gather(r, carry):
        total = [jnp.zeros((step_rows, seg), jnp.float32)] * targets
        total = add(total, out_slots[me, :, part(r), :], out_label[me])

        def one_source(i, running):
            source = (me + i) % owners
            slots_to(r, source, source).wait_recv()
            return tuple(add(list(running), in_slots[source, :, part(r), :], in_label[source]))

        total = lax.fori_loop(1, owners, one_source, tuple(total))
        for b in range(targets):
            sums[b, part(r), :] = total[b]
        return carry

    lax.fori_loop(0, GROUPS, gather, 0)

    for b in range(targets):
        high, low = split(sums[b])
        beam_ref[b * points : (b + 1) * points, :] = mm(steer_ref[b], high) + mm(steer_ref[b], low)

    def finish(i, carry):
        other = (me + i) % owners
        label_to(other, me).wait_send()
        for r in range(GROUPS):
            slots_to(r, other, me).wait_send()
        return carry

    lax.fori_loop(1, owners, finish, 0)
    for r in range(GROUPS):

        @pl.when(tm > 0)
        def _():
            to_after(r).wait_send()

        @pl.when(tm < ntm - 1)
        def _():
            to_prev(r).wait_send()


def copy_to(source, target, send, receive, place):
    return pltpu.make_async_remote_copy(
        src_ref=source,
        dst_ref=target,
        send_sem=send,
        recv_sem=receive,
        device_id=place,
        device_id_type=MESH,
    )


def line_kernel(
    dims,
    block_ref,
    owner_ref,
    sub_ref,
    delay_ref,
    frac_ref,
    record,
    taps_ref,
    table_ref,
    steer_ref,
    beam_ref,
    prev,
    after,
    band_hi,
    band_lo,
    tab,
    filt,
    shifted,
    held,
    names,
    out_slots,
    in_slots,
    out_label,
    in_label,
    out_dense,
    in_dense,
    sums,
    slot_pair,
    prev_send,
    prev_recv,
    after_send,
    after_recv,
    held_send,
    held_recv,
    name_send,
    name_recv,
    slot_send,
    slot_recv,
    label_send,
    label_recv,
    dense_send,
    dense_recv,
):
    nchan, nsrc, ntm = dims
    blocks, block_rows, seg = record.shape
    ntab, ntaps = taps_ref.shape
    pairs = block_ref.shape[0]
    cap = out_slots.shape[1]
    targets = steer_ref.shape[0]
    points = steer_ref.shape[1]
    step_rows = block_rows // PARTS
    rows = blocks * step_rows
    chip = lax.axis_index("chan")
    core = lax.axis_index("src")
    mate = 1 - core
    tm = lax.axis_index("tm")
    me = chip * nsrc + core
    middle = jnp.logical_and(chip > 0, chip < nchan - 1)
    ending = jnp.logical_or(chip == 0, chip == nchan - 1)
    low_half = chip < nchan // 2
    outer = jnp.where(low_half, 0, nchan - 1)
    inner = jnp.where(low_half, 1, nchan - 2)
    other = nchan - 1 - inner
    far = nchan - 1 - outer

    barrier = pltpu.get_barrier_semaphore()

    def greet(place):
        pl.semaphore_signal(barrier, inc=1, device_id=place, device_id_type=MESH)

    @pl.when(tm > 0)
    def _():
        greet({"tm": tm - 1})

    @pl.when(tm < ntm - 1)
    def _():
        greet({"tm": tm + 1})

    greet({"src": mate})

    @pl.when(middle)
    def _():
        greet({"chan": far, "src": core})
        greet({"chan": other, "src": core})
        greet({"chan": outer, "src": core})
        greet({"chan": outer, "src": mate})

    @pl.when(ending)
    def _():
        greet({"chan": other, "src": core})
        greet({"chan": inner, "src": core})
        greet({"chan": inner, "src": mate})

    build_band(taps_ref, band_hi, band_lo)

    @pl.when(tm == 0)
    def _():
        prev[...] = jnp.zeros_like(prev)

    @pl.when(tm == ntm - 1)
    def _():
        after[...] = jnp.zeros_like(after)

    pl.semaphore_wait(
        barrier,
        jnp.where(middle, 5, 4) + jnp.where(tm > 0, 1, 0) + jnp.where(tm < ntm - 1, 1, 0),
    )

    def part(r):
        return pl.ds(pl.multiple_of(r * step_rows, step_rows), step_rows)

    def to_prev(r):
        return copy_to(
            record.at[:, part(r), pl.ds(seg - ntaps, ntaps)],
            prev.at[:, part(r), :],
            prev_send.at[r],
            prev_recv.at[r],
            {"tm": tm + 1},
        )

    def to_after(r):
        return copy_to(
            record.at[:, part(r), :],
            after.at[:, part(r), :],
            after_send.at[r],
            after_recv.at[r],
            {"tm": tm - 1},
        )

    def held_to(kind, r, place):
        source = 2 if kind == 3 else 0
        return copy_to(
            held.at[pl.ds(source * pairs, pairs), part(r), :],
            held.at[pl.ds(kind * pairs, pairs), part(r), :],
            held_send.at[kind, r],
            held_recv.at[kind, r],
            place,
        )

    def name_to(kind, place):
        return copy_to(
            names.at[0], names.at[kind], name_send.at[kind], name_recv.at[kind], place
        )

    def slots_to(k, r, landing):
        return copy_to(
            out_slots.at[k, :, part(r), :],
            in_slots.at[landing, :, part(r), :],
            slot_send.at[k, r],
            slot_recv.at[landing, r],
            {"chan": outer, "src": k},
        )

    def label_to(k, landing):
        return copy_to(
            out_label.at[k],
            in_label.at[landing],
            label_send.at[k],
            label_recv.at[landing],
            {"chan": outer, "src": k},
        )

    def dense_to(k, r):
        return copy_to(
            out_dense.at[k, :, part(r), :],
            in_dense.at[:, part(r), :],
            dense_send.at[k, r],
            dense_recv.at[r],
            {"chan": far if k else other, "src": core},
        )

    for r in range(PARTS):

        @pl.when(tm > 0)
        def _():
            to_after(r).start()

        @pl.when(tm < ntm - 1)
        def _():
            to_prev(r).start()

    line = lax.broadcasted_iota(jnp.int32, (pairs, 128), 0)
    own_names = jnp.zeros((pairs, 128), jnp.int32)
    for p in range(pairs):
        own_names = jnp.where(line == p, owner_ref[p] * targets + sub_ref[p], own_names)
    names[0] = own_names.astype(jnp.float32)
    line = lax.broadcasted_iota(jnp.int32, out_label.shape[1:], 0)
    for k in range(nsrc):
        owner = outer * nsrc + k
        count = 0
        found = [-1] * cap
        for p in range(pairs):
            hit = owner_ref[p] == owner
            found = [jnp.where(jnp.logical_and(hit, count == j), p, found[j]) for j in range(cap)]
            count = count + jnp.where(hit, 1, 0)
        labels = jnp.full(out_label.shape[1:], -1, jnp.int32)
        for j in range(cap):
            pair = jnp.maximum(found[j], 0)
            slot_pair[k * cap + j] = pair
            name = jnp.where(found[j] >= 0, owner * targets + sub_ref[pair], -1)
            labels = jnp.where(line == j, name, labels)
        out_label[k] = labels.astype(jnp.float32)

    name_to(1, {"src": mate}).start()

    @pl.when(ending)
    def _():
        name_to(2, {"chan": inner, "src": core}).start()
        name_to(3, {"chan": inner, "src": mate}).start()

    @pl.when(middle)
    def _():
        for k in range(nsrc):
            label_to(k, core).start()

    for g in range(blocks):
        tab[g] = jnp.broadcast_to(table_ref[g : g + 1, :], (block_rows, block_rows)).T

    name_to(1, {"src": mate}).wait_recv()

    @pl.when(middle)
    def _():
        name_to(2, {"chan": inner, "src": core}).wait_recv()
        name_to(3, {"chan": inner, "src": mate}).wait_recv()

    @pl.when(ending)
    def _():
        for k in range(nsrc):
            label_to(k, k).wait_recv()

    def produce(r):
        @pl.when(tm > 0)
        def _():
            to_prev(r).wait_recv()

        @pl.when(tm < ntm - 1)
        def _():
            to_after(r).wait_recv()

        window = jnp.concatenate(
            [
                prev[:, part(r), :].reshape(rows, ntaps),
                record[:, part(r), :].reshape(rows, seg),
                after[:, part(r), :].reshape(rows, seg),
            ],
            axis=1,
        )
        inside = jnp.where(tm < ntm - 1, 1.0, 0.0)
        which = tab[:, part(r), :].reshape(rows, block_rows)
        band_filter(window, band_hi, band_lo, which, inside, seg, ntab, filt)

        def one_pair(p, c):
            value = shift_pair(filt[block_ref[p]], delay_ref[p], frac_ref[p], seg)
            held[p, part(r), :] = value
            shifted[p] = value
            return c

        lax.fori_loop(0, pairs, one_pair, 0, unroll=min(pairs, 4))
        held_to(1, r, {"src": mate}).start()

        @pl.when(ending)
        def _():
            held_to(2, r, {"chan": inner, "src": core}).start()

        @pl.when(middle)
        def _():
            for k in range(nsrc):
                for j in range(cap):
                    out_slots[k, j, part(r), :] = shifted[slot_pair[k * cap + j]]
                slots_to(k, r, core).start()

    def relay(r):
        held_to(2, r, {"chan": inner, "src": core}).wait_recv()
        held_to(3, r, {"src": mate}).start()

    def summed(r, first_names, kinds, depth):
        def one_kind(kind, running):
            total = list(running)
            for p in range(pairs):
                value = held[kind * pairs + p, part(r), :].astype(jnp.float32)
                name = names[kind, p : p + 1, :]
                name = jnp.concatenate([name] * (seg // 128), axis=1)
                for b in range(depth):
                    hit = name == first_names[b]
                    total[b] = total[b] + jnp.where(hit, value, 0.0)
            return tuple(total)

        empty = jnp.zeros((step_rows, seg), jnp.float32)
        return lax.fori_loop(0, kinds, one_kind, (empty,) * depth)

    def names_of(chan):
        start = (chan * nsrc + core) * targets
        return [(start + b).astype(jnp.float32) for b in range(targets)]

    def dense(r):
        held_to(1, r, {"src": mate}).wait_recv()
        held_to(3, r, {"src": mate}).wait_recv()
        wanted = names_of(far) + names_of(other)
        total = summed(r, wanted, 4, 2 * targets)
        for k, base in ((1, 0), (0, targets)):
            for b in range(targets):
                out_dense[k, b, part(r), :] = total[base + b].astype(jnp.bfloat16)
            dense_to(k, r).start()

    def produce_step(i, carry):
        @pl.when(i < PARTS)
        def _():
            produce(i)

        @pl.when(jnp.logical_and(middle, jnp.logical_and(i >= LAG, i < PARTS + LAG)))
        def _():
            relay(i - LAG)

        @pl.when(jnp.logical_and(middle, i >= LAG + MORE))
        def _():
            dense(i - LAG - MORE)

        return carry

    lax.fori_loop(0, PARTS + LAG + MORE, produce_step, 0)

    def finish(r, carry):
        @pl.when(ending)
        def _():
            held_to(1, r, {"src": mate}).wait_recv()

        mine = names_of(chip)
        total = summed(r, mine, jnp.where(middle, 4, 2), targets)
        for b in range(targets):
            sums[b, part(r), :] = total[b]

        @pl.when(ending)
        def _():
            total = [sums[b, part(r), :] for b in range(targets)]
            for k in range(nsrc):
                slots_to(k, r, k).wait_recv()
                for j in range(cap):
                    value = in_slots[k, j, part(r), :].astype(jnp.float32)
                    name = in_label[k, j : j + 1, :]
                    name = jnp.concatenate([name] * (seg // 128), axis=1)
                    total = [
                        total[b] + jnp.where(name == mine[b], value, 0.0) for b in range(targets)
                    ]
            for b in range(targets):
                sums[b, part(r), :] = total[b]

        dense_to(0, r).wait_recv()
        for b in range(targets):
            sums[b, part(r), :] = sums[b, part(r), :] + in_dense[b, part(r), :].astype(jnp.float32)
        return carry

    lax.fori_loop(0, PARTS, finish, 0)

    for b in range(targets):
        high, low = split(sums[b])
        beam_ref[b * points : (b + 1) * points, :] = mm(steer_ref[b], high) + mm(steer_ref[b], low)

    name_to(1, {"src": mate}).wait_send()

    @pl.when(ending)
    def _():
        name_to(2, {"chan": inner, "src": core}).wait_send()
        name_to(3, {"chan": inner, "src": mate}).wait_send()

    @pl.when(middle)
    def _():
        for k in range(nsrc):
            label_to(k, core).wait_send()

    def leave(r, carry):
        @pl.when(tm > 0)
        def _():
            to_after(r).wait_send()

        @pl.when(tm < ntm - 1)
        def _():
            to_prev(r).wait_send()

        held_to(1, r, {"src": mate}).wait_send()

        @pl.when(ending)
        def _():
            held_to(2, r, {"chan": inner, "src": core}).wait_send()

        @pl.when(middle)
        def _():
            held_to(3, r, {"src": mate}).wait_send()
            for k in range(nsrc):
                slots_to(k, r, core).wait_send()
            for k in range(2):
                dense_to(k, r).wait_send()

        return carry

    lax.fori_loop(0, PARTS, leave, 0)


def build_band(taps_ref, band_hi, band_lo):
    ntab, ntaps = taps_ref.shape
    for m in range(ntab):
        row = jnp.concatenate([taps_ref[m : m + 1, :], jnp.zeros((1, ntaps), jnp.float32)], axis=1)
        full = jnp.broadcast_to(row, (2 * ntaps, 2 * ntaps))
        rolled = pltpu.roll(full, ntaps, 1, stride=1, stride_axis=0)[:, :ntaps]
        high, low = split(rolled)
        band_hi[:, m * ntaps : (m + 1) * ntaps] = high
        band_lo[:, m * ntaps : (m + 1) * ntaps] = low


def band_filter(window, band_hi, band_lo, which, inside, seg, ntab, filt):
    blocks, step_rows, _ = filt.shape
    rows = blocks * step_rows
    ntaps = band_hi.shape[0] // 2
    high, low = split(window)
    steps = 2 * seg // ntaps
    lhs_hi = jnp.concatenate([high[:, j * ntaps : (j + 2) * ntaps] for j in range(steps)], axis=0)
    lhs_lo = jnp.concatenate([low[:, j * ntaps : (j + 2) * ntaps] for j in range(steps)], axis=0)
    every = mm(lhs_lo, band_hi[...]) + mm(lhs_hi, band_lo[...]) + mm(lhs_hi, band_hi[...])
    for j in range(steps):
        own = every[j * rows : (j + 1) * rows]
        value = own[:, :ntaps]
        for m in range(1, ntab):
            value = jnp.where(which == m, own[:, m * ntaps : (m + 1) * ntaps], value)
        if j >= seg // ntaps:
            value = value * inside
        filt[:, :, j * ntaps : (j + 1) * ntaps] = value.reshape(blocks, step_rows, ntaps)


def shift_pair(source, delay, frac, seg):
    mu = jnp.full((1, seg), frac.astype(jnp.float32)) / NFRAC
    first = -mu * (mu - 1.0) * (mu - 2.0) / 6.0
    second = (mu + 1.0) * (mu - 1.0) * (mu - 2.0) / 2.0
    third = -(mu + 1.0) * mu * (mu - 2.0) / 2.0
    fourth = (mu + 1.0) * mu * (mu - 1.0) / 6.0
    base = pltpu.roll(source, 2 * seg - (delay - 1), 1)
    mixed = first * base[:, :seg]
    mixed = mixed + second * pltpu.roll(base, 2 * seg - 1, 1)[:, :seg]
    mixed = mixed + third * pltpu.roll(base, 2 * seg - 2, 1)[:, :seg]
    mixed = mixed + fourth * pltpu.roll(base, 2 * seg - 3, 1)[:, :seg]
    return mixed.astype(jnp.bfloat16)


def solution(mesh):
    nchan, nsrc, ntm = mesh.shape["chan"], mesh.shape["src"], mesh.shape["tm"]
    owners = nchan * nsrc

    def local(
        record, fir_taps, chan_table, steering, pair_block, pair_owner, pair_sub, pair_delay, pair_frac
    ):
        channels, seg = record.shape
        ntab, ntaps = fir_taps.shape
        targets, points, block_rows = steering.shape
        blocks = channels // block_rows
        pairs = pair_block.shape[0]
        cap = 2 * pairs // owners
        step_rows = block_rows // GROUPS
        smem = pl.BlockSpec(memory_space=pltpu.SMEM)
        vmem = pl.BlockSpec(memory_space=pltpu.VMEM)
        dma = pltpu.SemaphoreType.DMA
        operands = (
            pair_block,
            pair_owner.reshape(pairs),
            pair_sub,
            pair_delay,
            pair_frac,
            record.reshape(blocks, block_rows, seg),
            fir_taps,
            chan_table.reshape(blocks, block_rows),
            steering,
        )
        if nchan == 4 and nsrc == 2:
            return pl.pallas_call(
                functools.partial(line_kernel, (nchan, nsrc, ntm)),
                out_shape=jax.ShapeDtypeStruct((targets * points, seg), jnp.float32),
                in_specs=[smem] * 5 + [vmem] * 4,
                out_specs=vmem,
                scratch_shapes=[
                    pltpu.VMEM((blocks, block_rows, ntaps), jnp.float32),
                    pltpu.VMEM((blocks, block_rows, seg), jnp.float32),
                    pltpu.VMEM((2 * ntaps, ntab * ntaps), jnp.bfloat16),
                    pltpu.VMEM((2 * ntaps, ntab * ntaps), jnp.bfloat16),
                    pltpu.VMEM((blocks, block_rows, block_rows), jnp.int32),
                    pltpu.VMEM((blocks, block_rows // PARTS, 2 * seg), jnp.float32),
                    pltpu.VMEM((pairs, block_rows // PARTS, seg), jnp.bfloat16),
                    pltpu.VMEM((4 * pairs, block_rows, seg), jnp.bfloat16),
                    pltpu.VMEM((4, pairs, 128), jnp.float32),
                    pltpu.VMEM((nsrc, cap, block_rows, seg), jnp.bfloat16),
                    pltpu.VMEM((nsrc, cap, block_rows, seg), jnp.bfloat16),
                    pltpu.VMEM((nsrc, 8, 128), jnp.float32),
                    pltpu.VMEM((nsrc, 8, 128), jnp.float32),
                    pltpu.VMEM((2, targets, block_rows, seg), jnp.bfloat16),
                    pltpu.VMEM((targets, block_rows, seg), jnp.bfloat16),
                    pltpu.VMEM((targets, block_rows, seg), jnp.float32),
                    pltpu.SMEM((nsrc * cap,), jnp.int32),
                    dma((PARTS,)),
                    dma((PARTS,)),
                    dma((PARTS,)),
                    dma((PARTS,)),
                    dma((4, PARTS)),
                    dma((4, PARTS)),
                    dma((4,)),
                    dma((4,)),
                    dma((nsrc, PARTS)),
                    dma((nsrc, PARTS)),
                    dma((nsrc,)),
                    dma((nsrc,)),
                    dma((2, PARTS)),
                    dma((PARTS,)),
                ],
                compiler_params=pltpu.CompilerParams(collective_id=0, has_side_effects=True),
            )(*operands)
        return pl.pallas_call(
            functools.partial(kernel, (nchan, nsrc, ntm)),
            out_shape=jax.ShapeDtypeStruct((targets * points, seg), jnp.float32),
            in_specs=[smem] * 5 + [vmem] * 4,
            out_specs=vmem,
            scratch_shapes=[
                pltpu.VMEM((blocks, block_rows, ntaps), jnp.float32),
                pltpu.VMEM((blocks, block_rows, seg), jnp.float32),
                pltpu.VMEM((2 * ntaps, ntab * ntaps), jnp.bfloat16),
                pltpu.VMEM((2 * ntaps, ntab * ntaps), jnp.bfloat16),
                pltpu.VMEM((blocks, block_rows, block_rows), jnp.int32),
                pltpu.VMEM((blocks, step_rows, 2 * seg), jnp.float32),
                pltpu.VMEM((pairs, step_rows, seg), jnp.bfloat16),
                pltpu.VMEM((owners, cap, block_rows, seg), jnp.bfloat16),
                pltpu.VMEM((owners, cap, block_rows, seg), jnp.bfloat16),
                pltpu.VMEM((owners, 8, 128), jnp.float32),
                pltpu.VMEM((owners, 8, 128), jnp.float32),
                pltpu.VMEM((targets, block_rows, seg), jnp.float32),
                pltpu.SMEM((owners * cap,), jnp.int32),
                dma((GROUPS,)),
                dma((GROUPS,)),
                dma((GROUPS,)),
                dma((GROUPS,)),
                dma((GROUPS, owners)),
                dma((GROUPS, owners)),
                dma((owners,)),
                dma((owners,)),
            ],
            compiler_params=pltpu.CompilerParams(collective_id=0, has_side_effects=True),
        )(*operands)

    in_specs = (
        P(("groups", "chan", "src"), "tm"),
        P(),
        P(("chan", "src")),
        P(("chan", "src"), None, None),
        P(("chan", "src")),
        P(("chan", "src"), None),
        P(("chan", "src")),
        P(("chan", "src")),
        P(("chan", "src")),
    )
    out_specs = P(("groups", "chan", "src"), "tm")
    return jax.shard_map(local, mesh=mesh, in_specs=in_specs, out_specs=out_specs, check_vma=False)
```

```python
import functools

import jax
import jax.numpy as jnp
from jax import lax
from jax.experimental import pallas as pl
from jax.experimental.pallas import tpu as pltpu
from jax.sharding import PartitionSpec as P

NFRAC = 16
GROUPS = 4
PARTS = 8
LAG = 2
MORE = 1
MESH = pl.DeviceIdType.MESH


def split(value):
    high = value.astype(jnp.bfloat16)
    return high, (value - high.astype(jnp.float32)).astype(jnp.bfloat16)


def mm(a, b):
    return jnp.dot(a, b, preferred_element_type=jnp.float32)


def kernel(
    dims,
    block_ref,
    owner_ref,
    sub_ref,
    delay_ref,
    frac_ref,
    record,
    taps_ref,
    table_ref,
    steer_ref,
    beam_ref,
    prev,
    after,
    band_hi,
    band_lo,
    tab,
    filt,
    shifted,
    out_slots,
    in_slots,
    out_label,
    in_label,
    sums,
    slot_pair,
    prev_send,
    prev_recv,
    after_send,
    after_recv,
    slot_send,
    slot_recv,
    label_send,
    label_recv,
):
    nchan, nsrc, ntm = dims
    owners = nchan * nsrc
    blocks, block_rows, seg = record.shape
    ntab, ntaps = taps_ref.shape
    pairs = block_ref.shape[0]
    cap = out_slots.shape[1]
    targets = steer_ref.shape[0]
    points = steer_ref.shape[1]
    step_rows = block_rows // GROUPS
    rows = blocks * step_rows
    me = lax.axis_index("chan") * nsrc + lax.axis_index("src")
    tm = lax.axis_index("tm")

    def place(owner):
        return {"chan": owner // nsrc, "src": owner % nsrc}

    barrier = pltpu.get_barrier_semaphore()

    @pl.when(tm > 0)
    def _():
        pl.semaphore_signal(barrier, inc=1, device_id={"tm": tm - 1}, device_id_type=MESH)

    @pl.when(tm < ntm - 1)
    def _():
        pl.semaphore_signal(barrier, inc=1, device_id={"tm": tm + 1}, device_id_type=MESH)

    def greet(i, carry):
        pl.semaphore_signal(
            barrier, inc=1, device_id=place((me + i) % owners), device_id_type=MESH
        )
        return carry

    lax.fori_loop(1, owners, greet, 0)

    build_band(taps_ref, band_hi, band_lo)

    @pl.when(tm == 0)
    def _():
        prev[...] = jnp.zeros_like(prev)

    @pl.when(tm == ntm - 1)
    def _():
        after[...] = jnp.zeros_like(after)

    pl.semaphore_wait(
        barrier,
        owners - 1 + jnp.where(tm > 0, 1, 0) + jnp.where(tm < ntm - 1, 1, 0),
    )

    def part(r):
        return pl.ds(pl.multiple_of(r * step_rows, step_rows), step_rows)

    def to_prev(r):
        return pltpu.make_async_remote_copy(
            src_ref=record.at[:, part(r), pl.ds(seg - ntaps, ntaps)],
            dst_ref=prev.at[:, part(r), :],
            send_sem=prev_send.at[r],
            recv_sem=prev_recv.at[r],
            device_id={"tm": tm + 1},
            device_id_type=MESH,
        )

    def to_after(r):
        return pltpu.make_async_remote_copy(
            src_ref=record.at[:, part(r), :],
            dst_ref=after.at[:, part(r), :],
            send_sem=after_send.at[r],
            recv_sem=after_recv.at[r],
            device_id={"tm": tm - 1},
            device_id_type=MESH,
        )

    def slots_to(r, other, landing):
        return pltpu.make_async_remote_copy(
            src_ref=out_slots.at[other, :, part(r), :],
            dst_ref=in_slots.at[landing, :, part(r), :],
            send_sem=slot_send.at[r, other],
            recv_sem=slot_recv.at[r, landing],
            device_id=place(other),
            device_id_type=MESH,
        )

    def label_to(other, landing):
        return pltpu.make_async_remote_copy(
            src_ref=out_label.at[other],
            dst_ref=in_label.at[landing],
            send_sem=label_send.at[other],
            recv_sem=label_recv.at[landing],
            device_id=place(other),
            device_id_type=MESH,
        )

    for r in range(GROUPS):

        @pl.when(tm > 0)
        def _():
            to_after(r).start()

        @pl.when(tm < ntm - 1)
        def _():
            to_prev(r).start()

    for g in range(blocks):
        tab[g] = jnp.broadcast_to(table_ref[g : g + 1, :], (block_rows, block_rows)).T

    def slots_of(owner, carry):
        def look(p, found):
            hit = owner_ref[p] == owner
            count = found[0]
            named = [
                jnp.where(jnp.logical_and(hit, count == k), p, found[1 + k]) for k in range(cap)
            ]
            return (count + jnp.where(hit, 1, 0), *named)

        found = lax.fori_loop(0, pairs, look, (0,) + (-1,) * cap, unroll=min(pairs, 8))
        line = lax.broadcasted_iota(jnp.int32, out_label.shape[1:], 0)
        labels = jnp.full(out_label.shape[1:], -1.0, jnp.float32)
        for k in range(cap):
            pair = jnp.maximum(found[1 + k], 0)
            slot_pair[owner * cap + k] = pair
            name = jnp.where(found[1 + k] >= 0, sub_ref[pair], -1).astype(jnp.float32)
            labels = jnp.where(line == k, name, labels)
        out_label[owner] = labels
        return carry

    lax.fori_loop(0, owners, slots_of, 0)

    def send_label(i, carry):
        label_to((me + i) % owners, me).start()
        return carry

    lax.fori_loop(1, owners, send_label, 0)

    def produce(r, carry):
        @pl.when(tm > 0)
        def _():
            to_prev(r).wait_recv()

        @pl.when(tm < ntm - 1)
        def _():
            to_after(r).wait_recv()

        window = jnp.concatenate(
            [
                prev[:, part(r), :].reshape(rows, ntaps),
                record[:, part(r), :].reshape(rows, seg),
                after[:, part(r), :].reshape(rows, seg),
            ],
            axis=1,
        )
        inside = jnp.where(tm < ntm - 1, 1.0, 0.0)
        which = tab[:, part(r), :].reshape(rows, block_rows)
        band_filter(window, band_hi, band_lo, which, inside, seg, ntab, filt)

        def one_pair(p, c):
            shifted[p] = shift_pair(filt[block_ref[p]], delay_ref[p], frac_ref[p], seg)
            return c

        lax.fori_loop(0, pairs, one_pair, 0, unroll=min(pairs, 4))

        def ship(i, c):
            other = (me + owners // 2 + i) % owners
            for k in range(cap):
                out_slots[other, k, part(r), :] = shifted[slot_pair[other * cap + k]]

            @pl.when(other != me)
            def _():
                slots_to(r, other, me).start()

            return c

        lax.fori_loop(0, owners, ship, 0)
        return carry

    lax.fori_loop(0, GROUPS, produce, 0)

    def wait_label(i, carry):
        source = (me + i) % owners
        label_to(source, source).wait_recv()
        return carry

    lax.fori_loop(1, owners, wait_label, 0)

    def add(total, values, labels):
        for k in range(cap):
            name = jnp.concatenate([labels[k : k + 1, :]] * (seg // labels.shape[1]), axis=1)
            value = values[k].astype(jnp.float32)
            total = [
                total[b] + value * jnp.where(name == float(b), 1.0, 0.0) for b in range(targets)
            ]
        return total

    def gather(r, carry):
        total = [jnp.zeros((step_rows, seg), jnp.float32)] * targets
        total = add(total, out_slots[me, :, part(r), :], out_label[me])

        def one_source(i, running):
            source = (me + i) % owners
            slots_to(r, source, source).wait_recv()
            return tuple(add(list(running), in_slots[source, :, part(r), :], in_label[source]))

        total = lax.fori_loop(1, owners, one_source, tuple(total))
        for b in range(targets):
            sums[b, part(r), :] = total[b]
        return carry

    lax.fori_loop(0, GROUPS, gather, 0)

    for b in range(targets):
        high, low = split(sums[b])
        beam_ref[b * points : (b + 1) * points, :] = mm(steer_ref[b], high) + mm(steer_ref[b], low)

    def finish(i, carry):
        other = (me + i) % owners
        label_to(other, me).wait_send()
        for r in range(GROUPS):
            slots_to(r, other, me).wait_send()
        return carry

    lax.fori_loop(1, owners, finish, 0)
    for r in range(GROUPS):

        @pl.when(tm > 0)
        def _():
            to_after(r).wait_send()

        @pl.when(tm < ntm - 1)
        def _():
            to_prev(r).wait_send()


def copy_to(source, target, send, receive, place):
    return pltpu.make_async_remote_copy(
        src_ref=source,
        dst_ref=target,
        send_sem=send,
        recv_sem=receive,
        device_id=place,
        device_id_type=MESH,
    )


def line_kernel(
    dims,
    block_ref,
    owner_ref,
    sub_ref,
    delay_ref,
    frac_ref,
    record,
    taps_ref,
    table_ref,
    sums,
    prev,
    after,
    band_hi,
    band_lo,
    tab,
    filt,
    shifted,
    held,
    names,
    out_slots,
    in_slots,
    out_label,
    in_label,
    out_dense,
    in_dense,
    slot_pair,
    prev_send,
    prev_recv,
    after_send,
    after_recv,
    held_send,
    held_recv,
    name_send,
    name_recv,
    slot_send,
    slot_recv,
    label_send,
    label_recv,
    dense_send,
    dense_recv,
):
    nchan, nsrc, ntm = dims
    blocks, block_rows, seg = record.shape
    ntab, ntaps = taps_ref.shape
    pairs = block_ref.shape[0]
    cap = out_slots.shape[1]
    targets = sums.shape[0]
    step_rows = block_rows // PARTS
    rows = blocks * step_rows
    chip = lax.axis_index("chan")
    core = lax.axis_index("src")
    mate = 1 - core
    tm = lax.axis_index("tm")
    me = chip * nsrc + core
    middle = jnp.logical_and(chip > 0, chip < nchan - 1)
    ending = jnp.logical_or(chip == 0, chip == nchan - 1)
    low_half = chip < nchan // 2
    outer = jnp.where(low_half, 0, nchan - 1)
    inner = jnp.where(low_half, 1, nchan - 2)
    other = nchan - 1 - inner
    far = nchan - 1 - outer

    barrier = pltpu.get_barrier_semaphore()

    def greet(place):
        pl.semaphore_signal(barrier, inc=1, device_id=place, device_id_type=MESH)

    @pl.when(tm > 0)
    def _():
        greet({"tm": tm - 1})

    @pl.when(tm < ntm - 1)
    def _():
        greet({"tm": tm + 1})

    greet({"src": mate})

    @pl.when(middle)
    def _():
        greet({"chan": far, "src": core})
        greet({"chan": other, "src": core})
        greet({"chan": outer, "src": core})
        greet({"chan": outer, "src": mate})

    @pl.when(ending)
    def _():
        greet({"chan": other, "src": core})
        greet({"chan": inner, "src": core})
        greet({"chan": inner, "src": mate})

    build_band(taps_ref, band_hi, band_lo)

    @pl.when(tm == 0)
    def _():
        prev[...] = jnp.zeros_like(prev)

    @pl.when(tm == ntm - 1)
    def _():
        after[...] = jnp.zeros_like(after)

    pl.semaphore_wait(
        barrier,
        jnp.where(middle, 5, 4) + jnp.where(tm > 0, 1, 0) + jnp.where(tm < ntm - 1, 1, 0),
    )

    def part(r):
        return pl.ds(pl.multiple_of(r * step_rows, step_rows), step_rows)

    def to_prev(r):
        return copy_to(
            record.at[:, part(r), pl.ds(seg - ntaps, ntaps)],
            prev.at[:, part(r), :],
            prev_send.at[r],
            prev_recv.at[r],
            {"tm": tm + 1},
        )

    def to_after(r):
        return copy_to(
            record.at[:, part(r), :],
            after.at[:, part(r), :],
            after_send.at[r],
            after_recv.at[r],
            {"tm": tm - 1},
        )

    def held_to(kind, r, place):
        source = 2 if kind == 3 else 0
        return copy_to(
            held.at[pl.ds(source * pairs, pairs), part(r), :],
            held.at[pl.ds(kind * pairs, pairs), part(r), :],
            held_send.at[kind, r],
            held_recv.at[kind, r],
            place,
        )

    def name_to(kind, place):
        return copy_to(
            names.at[0], names.at[kind], name_send.at[kind], name_recv.at[kind], place
        )

    def slots_to(k, r, landing):
        return copy_to(
            out_slots.at[k, :, part(r), :],
            in_slots.at[landing, :, part(r), :],
            slot_send.at[k, r],
            slot_recv.at[landing, r],
            {"chan": outer, "src": k},
        )

    def label_to(k, landing):
        return copy_to(
            out_label.at[k],
            in_label.at[landing],
            label_send.at[k],
            label_recv.at[landing],
            {"chan": outer, "src": k},
        )

    def dense_to(k, r):
        return copy_to(
            out_dense.at[k, :, part(r), :],
            in_dense.at[:, part(r), :],
            dense_send.at[k, r],
            dense_recv.at[r],
            {"chan": far if k else other, "src": core},
        )

    for r in range(PARTS):

        @pl.when(tm > 0)
        def _():
            to_after(r).start()

        @pl.when(tm < ntm - 1)
        def _():
            to_prev(r).start()

    line = lax.broadcasted_iota(jnp.int32, (pairs, 128), 0)
    own_names = jnp.zeros((pairs, 128), jnp.int32)
    for p in range(pairs):
        own_names = jnp.where(line == p, owner_ref[p] * targets + sub_ref[p], own_names)
    names[0] = own_names.astype(jnp.float32)
    line = lax.broadcasted_iota(jnp.int32, out_label.shape[1:], 0)
    for k in range(nsrc):
        owner = outer * nsrc + k
        count = 0
        found = [-1] * cap
        for p in range(pairs):
            hit = owner_ref[p] == owner
            found = [jnp.where(jnp.logical_and(hit, count == j), p, found[j]) for j in range(cap)]
            count = count + jnp.where(hit, 1, 0)
        labels = jnp.full(out_label.shape[1:], -1, jnp.int32)
        for j in range(cap):
            pair = jnp.maximum(found[j], 0)
            slot_pair[k * cap + j] = pair
            name = jnp.where(found[j] >= 0, owner * targets + sub_ref[pair], -1)
            labels = jnp.where(line == j, name, labels)
        out_label[k] = labels.astype(jnp.float32)

    name_to(1, {"src": mate}).start()

    @pl.when(ending)
    def _():
        name_to(2, {"chan": inner, "src": core}).start()
        name_to(3, {"chan": inner, "src": mate}).start()

    @pl.when(middle)
    def _():
        for k in range(nsrc):
            label_to(k, core).start()

    for g in range(blocks):
        tab[g] = jnp.broadcast_to(table_ref[g : g + 1, :], (block_rows, block_rows)).T

    name_to(1, {"src": mate}).wait_recv()

    @pl.when(middle)
    def _():
        name_to(2, {"chan": inner, "src": core}).wait_recv()
        name_to(3, {"chan": inner, "src": mate}).wait_recv()

    @pl.when(ending)
    def _():
        for k in range(nsrc):
            label_to(k, k).wait_recv()

    def produce(r):
        @pl.when(tm > 0)
        def _():
            to_prev(r).wait_recv()

        @pl.when(tm < ntm - 1)
        def _():
            to_after(r).wait_recv()

        window = jnp.concatenate(
            [
                prev[:, part(r), :].reshape(rows, ntaps),
                record[:, part(r), :].reshape(rows, seg),
                after[:, part(r), :].reshape(rows, seg),
            ],
            axis=1,
        )
        inside = jnp.where(tm < ntm - 1, 1.0, 0.0)
        which = tab[:, part(r), :].reshape(rows, block_rows)
        band_filter(window, band_hi, band_lo, which, inside, seg, ntab, filt)

        def one_pair(p, c):
            value = shift_pair(filt[block_ref[p]], delay_ref[p], frac_ref[p], seg)
            held[p, part(r), :] = value
            shifted[p] = value
            return c

        lax.fori_loop(0, pairs, one_pair, 0, unroll=min(pairs, 4))
        held_to(1, r, {"src": mate}).start()

        @pl.when(ending)
        def _():
            held_to(2, r, {"chan": inner, "src": core}).start()

        @pl.when(middle)
        def _():
            for k in range(nsrc):
                for j in range(cap):
                    out_slots[k, j, part(r), :] = shifted[slot_pair[k * cap + j]]
                slots_to(k, r, core).start()

    def relay(r):
        held_to(2, r, {"chan": inner, "src": core}).wait_recv()
        held_to(3, r, {"src": mate}).start()

    def summed(r, first_names, kinds, depth):
        def one_kind(kind, running):
            total = list(running)
            for p in range(pairs):
                value = held[kind * pairs + p, part(r), :].astype(jnp.float32)
                name = names[kind, p : p + 1, :]
                name = jnp.concatenate([name] * (seg // 128), axis=1)
                for b in range(depth):
                    hit = name == first_names[b]
                    total[b] = total[b] + jnp.where(hit, value, 0.0)
            return tuple(total)

        empty = jnp.zeros((step_rows, seg), jnp.float32)
        return lax.fori_loop(0, kinds, one_kind, (empty,) * depth)

    def names_of(chan):
        start = (chan * nsrc + core) * targets
        return [(start + b).astype(jnp.float32) for b in range(targets)]

    def dense(r):
        held_to(1, r, {"src": mate}).wait_recv()
        held_to(3, r, {"src": mate}).wait_recv()
        wanted = names_of(far) + names_of(other)
        total = summed(r, wanted, 4, 2 * targets)
        for k, base in ((1, 0), (0, targets)):
            for b in range(targets):
                out_dense[k, b, part(r), :] = total[base + b].astype(jnp.bfloat16)
            dense_to(k, r).start()

    def produce_step(i, carry):
        @pl.when(i < PARTS)
        def _():
            produce(i)

        @pl.when(jnp.logical_and(middle, jnp.logical_and(i >= LAG, i < PARTS + LAG)))
        def _():
            relay(i - LAG)

        @pl.when(jnp.logical_and(middle, i >= LAG + MORE))
        def _():
            dense(i - LAG - MORE)

        return carry

    lax.fori_loop(0, PARTS + LAG + MORE, produce_step, 0)

    def finish(r, carry):
        @pl.when(ending)
        def _():
            held_to(1, r, {"src": mate}).wait_recv()

        mine = names_of(chip)
        total = summed(r, mine, jnp.where(middle, 4, 2), targets)
        for b in range(targets):
            sums[b, part(r), :] = total[b]

        @pl.when(ending)
        def _():
            total = [sums[b, part(r), :] for b in range(targets)]
            for k in range(nsrc):
                slots_to(k, r, k).wait_recv()
                for j in range(cap):
                    value = in_slots[k, j, part(r), :].astype(jnp.float32)
                    name = in_label[k, j : j + 1, :]
                    name = jnp.concatenate([name] * (seg // 128), axis=1)
                    total = [
                        total[b] + jnp.where(name == mine[b], value, 0.0) for b in range(targets)
                    ]
            for b in range(targets):
                sums[b, part(r), :] = total[b]

        dense_to(0, r).wait_recv()
        for b in range(targets):
            sums[b, part(r), :] = sums[b, part(r), :] + in_dense[b, part(r), :].astype(jnp.float32)
        return carry

    lax.fori_loop(0, PARTS, finish, 0)

    name_to(1, {"src": mate}).wait_send()

    @pl.when(ending)
    def _():
        name_to(2, {"chan": inner, "src": core}).wait_send()
        name_to(3, {"chan": inner, "src": mate}).wait_send()

    @pl.when(middle)
    def _():
        for k in range(nsrc):
            label_to(k, core).wait_send()

    def leave(r, carry):
        @pl.when(tm > 0)
        def _():
            to_after(r).wait_send()

        @pl.when(tm < ntm - 1)
        def _():
            to_prev(r).wait_send()

        held_to(1, r, {"src": mate}).wait_send()

        @pl.when(ending)
        def _():
            held_to(2, r, {"chan": inner, "src": core}).wait_send()

        @pl.when(middle)
        def _():
            held_to(3, r, {"src": mate}).wait_send()
            for k in range(nsrc):
                slots_to(k, r, core).wait_send()
            for k in range(2):
                dense_to(k, r).wait_send()

        return carry

    lax.fori_loop(0, PARTS, leave, 0)


def build_band(taps_ref, band_hi, band_lo):
    ntab, ntaps = taps_ref.shape
    for m in range(ntab):
        row = jnp.concatenate([taps_ref[m : m + 1, :], jnp.zeros((1, ntaps), jnp.float32)], axis=1)
        full = jnp.broadcast_to(row, (2 * ntaps, 2 * ntaps))
        rolled = pltpu.roll(full, ntaps, 1, stride=1, stride_axis=0)[:, :ntaps]
        high, low = split(rolled)
        band_hi[:, m * ntaps : (m + 1) * ntaps] = high
        band_lo[:, m * ntaps : (m + 1) * ntaps] = low


def band_filter(window, band_hi, band_lo, which, inside, seg, ntab, filt):
    blocks, step_rows, _ = filt.shape
    rows = blocks * step_rows
    ntaps = band_hi.shape[0] // 2
    high, low = split(window)
    steps = 2 * seg // ntaps
    lhs_hi = jnp.concatenate([high[:, j * ntaps : (j + 2) * ntaps] for j in range(steps)], axis=0)
    lhs_lo = jnp.concatenate([low[:, j * ntaps : (j + 2) * ntaps] for j in range(steps)], axis=0)
    every = mm(lhs_lo, band_hi[...]) + mm(lhs_hi, band_lo[...]) + mm(lhs_hi, band_hi[...])
    for j in range(steps):
        own = every[j * rows : (j + 1) * rows]
        value = own[:, :ntaps]
        for m in range(1, ntab):
            value = jnp.where(which == m, own[:, m * ntaps : (m + 1) * ntaps], value)
        if j >= seg // ntaps:
            value = value * inside
        filt[:, :, j * ntaps : (j + 1) * ntaps] = value.reshape(blocks, step_rows, ntaps)


def shift_pair(source, delay, frac, seg):
    mu = jnp.full((1, seg), frac.astype(jnp.float32)) / NFRAC
    first = -mu * (mu - 1.0) * (mu - 2.0) / 6.0
    second = (mu + 1.0) * (mu - 1.0) * (mu - 2.0) / 2.0
    third = -(mu + 1.0) * mu * (mu - 2.0) / 2.0
    fourth = (mu + 1.0) * mu * (mu - 1.0) / 6.0
    base = pltpu.roll(source, 2 * seg - (delay - 1), 1)
    mixed = first * base[:, :seg]
    mixed = mixed + second * pltpu.roll(base, 2 * seg - 1, 1)[:, :seg]
    mixed = mixed + third * pltpu.roll(base, 2 * seg - 2, 1)[:, :seg]
    mixed = mixed + fourth * pltpu.roll(base, 2 * seg - 3, 1)[:, :seg]
    return mixed.astype(jnp.bfloat16)


def solution(mesh):
    nchan, nsrc, ntm = mesh.shape["chan"], mesh.shape["src"], mesh.shape["tm"]
    owners = nchan * nsrc

    def local(
        record, fir_taps, chan_table, steering, pair_block, pair_owner, pair_sub, pair_delay, pair_frac
    ):
        channels, seg = record.shape
        ntab, ntaps = fir_taps.shape
        targets, points, block_rows = steering.shape
        blocks = channels // block_rows
        pairs = pair_block.shape[0]
        cap = 2 * pairs // owners
        step_rows = block_rows // GROUPS
        smem = pl.BlockSpec(memory_space=pltpu.SMEM)
        vmem = pl.BlockSpec(memory_space=pltpu.VMEM)
        dma = pltpu.SemaphoreType.DMA
        operands = (
            pair_block,
            pair_owner.reshape(pairs),
            pair_sub,
            pair_delay,
            pair_frac,
            record.reshape(blocks, block_rows, seg),
            fir_taps,
            chan_table.reshape(blocks, block_rows),
            steering,
        )
        if nchan == 4 and nsrc == 2:
            sums = pl.pallas_call(
                functools.partial(line_kernel, (nchan, nsrc, ntm)),
                out_shape=jax.ShapeDtypeStruct((targets, block_rows, seg), jnp.float32),
                in_specs=[smem] * 5 + [vmem] * 3,
                out_specs=vmem,
                scratch_shapes=[
                    pltpu.VMEM((blocks, block_rows, ntaps), jnp.float32),
                    pltpu.VMEM((blocks, block_rows, seg), jnp.float32),
                    pltpu.VMEM((2 * ntaps, ntab * ntaps), jnp.bfloat16),
                    pltpu.VMEM((2 * ntaps, ntab * ntaps), jnp.bfloat16),
                    pltpu.VMEM((blocks, block_rows, block_rows), jnp.int32),
                    pltpu.VMEM((blocks, block_rows // PARTS, 2 * seg), jnp.float32),
                    pltpu.VMEM((pairs, block_rows // PARTS, seg), jnp.bfloat16),
                    pltpu.VMEM((4 * pairs, block_rows, seg), jnp.bfloat16),
                    pltpu.VMEM((4, pairs, 128), jnp.float32),
                    pltpu.VMEM((nsrc, cap, block_rows, seg), jnp.bfloat16),
                    pltpu.VMEM((nsrc, cap, block_rows, seg), jnp.bfloat16),
                    pltpu.VMEM((nsrc, 8, 128), jnp.float32),
                    pltpu.VMEM((nsrc, 8, 128), jnp.float32),
                    pltpu.VMEM((2, targets, block_rows, seg), jnp.bfloat16),
                    pltpu.VMEM((targets, block_rows, seg), jnp.bfloat16),
                    pltpu.SMEM((nsrc * cap,), jnp.int32),
                    dma((PARTS,)),
                    dma((PARTS,)),
                    dma((PARTS,)),
                    dma((PARTS,)),
                    dma((4, PARTS)),
                    dma((4, PARTS)),
                    dma((4,)),
                    dma((4,)),
                    dma((nsrc, PARTS)),
                    dma((nsrc, PARTS)),
                    dma((nsrc,)),
                    dma((nsrc,)),
                    dma((2, PARTS)),
                    dma((PARTS,)),
                ],
                compiler_params=pltpu.CompilerParams(collective_id=0, has_side_effects=True),
            )(*operands[:-1])
            beam = jnp.einsum(
                "bxc,bct->bxt",
                steering.astype(jnp.float32),
                sums,
                precision=lax.Precision.HIGHEST,
            )
            return beam.reshape(targets * points, seg)
        return pl.pallas_call(
            functools.partial(kernel, (nchan, nsrc, ntm)),
            out_shape=jax.ShapeDtypeStruct((targets * points, seg), jnp.float32),
            in_specs=[smem] * 5 + [vmem] * 4,
            out_specs=vmem,
            scratch_shapes=[
                pltpu.VMEM((blocks, block_rows, ntaps), jnp.float32),
                pltpu.VMEM((blocks, block_rows, seg), jnp.float32),
                pltpu.VMEM((2 * ntaps, ntab * ntaps), jnp.bfloat16),
                pltpu.VMEM((2 * ntaps, ntab * ntaps), jnp.bfloat16),
                pltpu.VMEM((blocks, block_rows, block_rows), jnp.int32),
                pltpu.VMEM((blocks, step_rows, 2 * seg), jnp.float32),
                pltpu.VMEM((pairs, step_rows, seg), jnp.bfloat16),
                pltpu.VMEM((owners, cap, block_rows, seg), jnp.bfloat16),
                pltpu.VMEM((owners, cap, block_rows, seg), jnp.bfloat16),
                pltpu.VMEM((owners, 8, 128), jnp.float32),
                pltpu.VMEM((owners, 8, 128), jnp.float32),
                pltpu.VMEM((targets, block_rows, seg), jnp.float32),
                pltpu.SMEM((owners * cap,), jnp.int32),
                dma((GROUPS,)),
                dma((GROUPS,)),
                dma((GROUPS,)),
                dma((GROUPS,)),
                dma((GROUPS, owners)),
                dma((GROUPS, owners)),
                dma((owners,)),
                dma((owners,)),
            ],
            compiler_params=pltpu.CompilerParams(collective_id=0, has_side_effects=True),
        )(*operands)

    in_specs = (
        P(("groups", "chan", "src"), "tm"),
        P(),
        P(("chan", "src")),
        P(("chan", "src"), None, None),
        P(("chan", "src")),
        P(("chan", "src"), None),
        P(("chan", "src")),
        P(("chan", "src")),
        P(("chan", "src")),
    )
    out_specs = P(("groups", "chan", "src"), "tm")
    return jax.shard_map(local, mesh=mesh, in_specs=in_specs, out_specs=out_specs, check_vma=False)
```
